32 devices in a mesh: fsdp: 16 (over z, y, x), tensor: 2 (over core).
Axes of the slice: x: 2, y: 2, z: 4, core: 2. Of those that a mesh axis runs over, the one named last changes fastest.
Arguments:
- images: bfloat16 [16, 577, 1024], P('fsdp'), may hold values from -6 to 6
- out_cotangent: bfloat16 [16, 577, 1024], P('fsdp'), may hold values from -6 to 6
- qkv_weight: bfloat16 [1024, 3, 1024], P('fsdp', None, 'tensor'), may hold values from -0.1875 to 0.1875
- out_weight: bfloat16 [1024, 1024], P('fsdp', 'tensor'), may hold values from -1.5 to 1.5
- up_weight: bfloat16 [1024, 4096], P('fsdp', 'tensor'), may hold values from -0.1875 to 0.1875
- down_weight: bfloat16 [1024, 4096], P('fsdp', 'tensor'), may hold values from -0.09375 to 0.09375
- norm_gain: float32 [2, 1024], replicated, may hold values from 0.1 to 1.9
- norm_bias: float32 [2, 1024], replicated, may hold values from -2 to 2
- attn_bias: float32 [2, 1024], P(None, 'tensor'), may hold values from -2 to 2
- res_bias: float32 [2, 1024], replicated, may hold values from -2 to 2
- up_bias: float32 [4096], P('tensor'), may hold values from -2 to 2
- qkv_moment: float32 [1024, 3, 1024], P('fsdp', None, 'tensor'), may hold values from -512 to 512
- out_moment: float32 [1024, 1024], P('fsdp', 'tensor'), may hold values from -512 to 512
- up_moment: float32 [1024, 4096], P('fsdp', 'tensor'), may hold values from -512 to 512
- down_moment: float32 [1024, 4096], P('fsdp', 'tensor'), may hold values from -512 to 512
- gain_moment: float32 [2, 1024], replicated, may hold values from -512 to 512
- nbias_moment: float32 [2, 1024], replicated, may hold values from -512 to 512
- abias_moment: float32 [2, 1024], P(None, 'tensor'), may hold values from -512 to 512
- rbias_moment: float32 [2, 1024], replicated, may hold values from -512 to 512
- ubias_moment: float32 [4096], P('tensor'), may hold values from -512 to 512
Outputs:
- block_out: bfloat16 [16, 577, 1024], P('fsdp')
- images_grad: float32 [16, 577, 1024], P('fsdp')
- qkv_weight_grad: float32 [1024, 3, 1024], P('fsdp', None, 'tensor')
- out_weight_grad: float32 [1024, 1024], P('fsdp', 'tensor')
- up_weight_grad: float32 [1024, 4096], P('fsdp', 'tensor')
- down_weight_grad: float32 [1024, 4096], P('fsdp', 'tensor')
- norm_gain_grad: float32 [2, 1024], replicated
- norm_bias_grad: float32 [2, 1024], replicated
- attn_bias_grad: float32 [2, 1024], P(None, 'tensor')
- res_bias_grad: float32 [2, 1024], replicated
- up_bias_grad: float32 [4096], P('tensor')
- qkv_weight_new: float32 [1024, 3, 1024], P('fsdp', None, 'tensor')
- out_weight_new: float32 [1024, 1024], P('fsdp', 'tensor')
- up_weight_new: float32 [1024, 4096], P('fsdp', 'tensor')
- down_weight_new: float32 [1024, 4096], P('fsdp', 'tensor')
- norm_gain_new: float32 [2, 1024], replicated
- norm_bias_new: float32 [2, 1024], replicated
- attn_bias_new: float32 [2, 1024], P(None, 'tensor')
- res_bias_new: float32 [2, 1024], replicated
- up_bias_new: float32 [4096], P('tensor')
- qkv_moment_new: float32 [1024, 3, 1024], P('fsdp', None, 'tensor')
- out_moment_new: float32 [1024, 1024], P('fsdp', 'tensor')
- up_moment_new: float32 [1024, 4096], P('fsdp', 'tensor')
- down_moment_new: float32 [1024, 4096], P('fsdp', 'tensor')
- gain_moment_new: float32 [2, 1024], replicated
- nbias_moment_new: float32 [2, 1024], replicated
- abias_moment_new: float32 [2, 1024], P(None, 'tensor')
- rbias_moment_new: float32 [2, 1024], replicated
- ubias_moment_new: float32 [4096], P('tensor')
The draws below stay inside these ranges and needn't reach their ends.
All inputs are finite; a program needn't handle non-finite values.
Results may differ from the reference program's by a relative error of at most 0.013.
Values may be sent and summed in bfloat16 or wider, within the bound.
No kernel may reach another device: no remote copies, remote signals or barrier semaphores. Data moves between devices by JAX's collectives and lax.ppermute only.
A program may use at most 256 MiB of HBM per device.

```python
import math
import jax
import jax.numpy as jnp
from jax import lax

D = 1024
HEADS = 16
HEAD_DIM = 64
FF = 4096
SEQ = 577
NS_STEPS = 5
IMAGES = 16
N_TENSOR = 2


def block_levels(own_key, dims, split, least, top_value):
    def one(dim, parts):
        heights = jax.random.uniform(jax.random.fold_in(jax.random.fold_in(own_key, 6), dim), (parts,), jnp.float32, least / len(split), top_value / len(split))
        return jnp.repeat(jnp.exp(heights), dims[dim] // parts).reshape((-1,) + (1,) * (len(dims) - dim - 1))

    factor_of = one(*split[0])
    for cut in split[1:]:
        factor_of = factor_of * one(*cut)
    return factor_of


def gaussian(stream_key, dims, deviation, bound, cuts=(), dtype=jnp.bfloat16):
    array = jax.random.normal(stream_key, dims, jnp.float32) * deviation
    if len(cuts) > 0:
        array = block_levels(stream_key, dims, cuts, -0.22, 0.18) * array
    return jnp.clip(array, min=-bound, max=bound).astype(dtype)


def setup_inputs(seed: int = 0) -> dict:
    splits = jax.random.split(jax.random.key(seed), 21)
    return {
        "images": gaussian(splits[0], (IMAGES, SEQ, D), 1.0, 6.0, ((0, 16),)),
        "out_cotangent": gaussian(splits[1], (IMAGES, SEQ, D), 1.0, 6.0, ((0, 16),)),
        "qkv_weight": gaussian(splits[2], (D, 3, D), D ** -0.5, 0.1875, ((0, 16), (2, 2))),
        "out_weight": gaussian(splits[3], (D, D), (D // 64) ** -0.5, 1.5, ((0, 16), (1, 2))),
        "up_weight": gaussian(splits[4], (D, FF), D ** -0.5, 0.1875, ((0, 16), (1, 2))),
        "down_weight": gaussian(splits[5], (D, FF), FF ** -0.5, 0.09375, ((0, 16), (1, 2))),
        "norm_gain": jnp.clip(1.0 + 0.18 * jax.random.normal(splits[6], (2, D), jnp.float32), 0.1, 1.9),
        "norm_bias": gaussian(splits[7], (2, D), 0.3, 2.0, (), jnp.float32),
        "attn_bias": gaussian(splits[8], (2, D), 0.3, 2.0, ((1, 2),), jnp.float32),
        "res_bias": gaussian(splits[9], (2, D), 0.3, 2.0, (), jnp.float32),
        "up_bias": gaussian(splits[10], (FF,), 0.3, 2.0, ((0, 2),), jnp.float32),
        "qkv_moment": gaussian(splits[11], (D, 3, D), ((IMAGES * SEQ) ** 0.5), 512.0, ((0, 16), (2, 2)), jnp.float32),
        "out_moment": gaussian(splits[12], (D, D), ((IMAGES * SEQ) ** 0.5), 512.0, ((0, 16), (1, 2)), jnp.float32),
        "up_moment": gaussian(splits[13], (D, FF), ((IMAGES * SEQ) ** 0.5), 512.0, ((0, 16), (1, 2)), jnp.float32),
        "down_moment": gaussian(splits[14], (D, FF), ((IMAGES * SEQ) ** 0.5), 512.0, ((0, 16), (1, 2)), jnp.float32),
        "gain_moment": gaussian(splits[15], (2, D), ((IMAGES * SEQ) ** 0.5), 512.0, (), jnp.float32),
        "nbias_moment": gaussian(splits[16], (2, D), ((IMAGES * SEQ) ** 0.5), 512.0, (), jnp.float32),
        "abias_moment": gaussian(splits[17], (2, D), ((IMAGES * SEQ) ** 0.5), 512.0, ((1, 2),), jnp.float32),
        "rbias_moment": gaussian(splits[18], (2, D), ((IMAGES * SEQ) ** 0.5), 512.0, (), jnp.float32),
        "ubias_moment": gaussian(splits[19], (FF,), ((IMAGES * SEQ) ** 0.5), 512.0, ((0, 2),), jnp.float32),
    }


@jax.custom_vjp
def low(v):
    return lax.optimization_barrier(v.astype(jnp.bfloat16)).astype(jnp.float32)

@jax.custom_vjp
def low_back(v):
    return v

def low_keep(v):
    return (low(v), None)

def low_pass(kept, grad):
    return (grad,)

def back_keep(v):
    return (v, None)

def back_low(kept, grad):
    return (low(grad),)
low.defvjp(low_keep, low_pass)
low_back.defvjp(back_keep, back_low)
HIGHEST = lax.Precision.HIGHEST
LN_EPS = 1e-06
NS_EPS = 1e-06
COEF_A = 3.4445
COEF_B = -4.775
COEF_C = 2.0315
MOMENTUM = 0.95
MUON_RATE = 0.15
VECTOR_RATE = 0.002
ROOT_HALF = 0.7071067811865476

def layer_norm(values, gain, shift):
    center = values - lax.optimization_barrier(jnp.mean(values, axis=-1, keepdims=True))
    inverse = lax.rsqrt(lax.optimization_barrier(jnp.mean(center * center, axis=-1, keepdims=True)) + LN_EPS)
    return center * inverse * gain + shift

def gelu_value(upper):
    return 0.5 * upper * (1.0 + jax.scipy.special.erf(upper * ROOT_HALF))

def image_layer(params, rows_x):
    qkv_matrix, out_matrix, up_matrix, down_matrix, gains, shifts, attn_shift, res_shift, up_shift = params
    normed1 = low(layer_norm(rows_x, gains[0], shifts[0]))
    proj = jnp.einsum('td,djh->tjh', normed1, qkv_matrix, precision=HIGHEST)
    bias_three = jnp.stack([attn_shift[0], jnp.zeros_like(attn_shift[0]), attn_shift[1]])
    proj = low(low_back(proj + bias_three))
    length = rows_x.shape[0]
    queries = proj[:, 0].reshape(length, HEADS, HEAD_DIM)
    keys_all = proj[:, 1].reshape(length, HEADS, HEAD_DIM)
    values_all = proj[:, 2].reshape(length, HEADS, HEAD_DIM)
    scores = jnp.einsum('qhe,khe->hqk', queries, keys_all, precision=HIGHEST) * HEAD_DIM ** (-0.5)
    scores = low_back(scores)
    ceiling = lax.optimization_barrier(jnp.max(scores, axis=-1, keepdims=True))
    exponent = jnp.exp(scores - ceiling)
    probs = low(exponent / lax.optimization_barrier(jnp.sum(exponent, axis=-1, keepdims=True)))
    attn = jnp.einsum('hqk,khe->qhe', probs, values_all, precision=HIGHEST).reshape(length, D)
    attn = low(low_back(attn))
    branch = low_back(jnp.dot(attn, out_matrix.T, precision=HIGHEST))
    mid = rows_x + branch + res_shift[0]
    normed2 = low(layer_norm(mid, gains[1], shifts[1]))
    upper = low_back(jnp.dot(normed2, up_matrix, precision=HIGHEST) + up_shift)
    hidden = low(gelu_value(upper))
    second = low_back(jnp.dot(hidden, down_matrix.T, precision=HIGHEST))
    return mid + second + res_shift[1]

def forward(params, inputs):
    stepper = jax.checkpoint(lambda rows_x: image_layer(params, rows_x))
    return lax.map(stepper, inputs)

def orthogonal(matrix):
    rows, cols = matrix.shape
    current = matrix.astype(jnp.float32)
    if rows > cols:
        current = current.T
    norm_value = jnp.sqrt(jnp.sum(current * current))
    current = current / (norm_value + NS_EPS)
    for repeat in range(NS_STEPS):
        gram = jnp.dot(current, current.T, precision=HIGHEST)
        poly = COEF_B * gram + COEF_C * jnp.dot(gram, gram, precision=HIGHEST)
        current = COEF_A * current + jnp.dot(poly, current, precision=HIGHEST)
    if rows > cols:
        current = current.T
    return current

def muon_matrix(weight, moment_new):
    cols = moment_new.shape[1]
    blockwidth = cols // N_TENSOR
    pieces = []
    for column in range(N_TENSOR):
        block = moment_new[:, column * blockwidth:(column + 1) * blockwidth].astype(jnp.bfloat16)
        orth = orthogonal(block)
        pieces.append(orth * (0.2 * math.sqrt(max(moment_new.shape[0], blockwidth))))
    update = jnp.concatenate(pieces, axis=1)
    return weight.astype(jnp.float32) - MUON_RATE * update

def reference(images, out_cotangent, qkv_weight, out_weight, up_weight, down_weight, norm_gain, norm_bias, attn_bias, res_bias, up_bias, qkv_moment, out_moment, up_moment, down_moment, gain_moment, nbias_moment, abias_moment, rbias_moment, ubias_moment):
    params = (qkv_weight.astype(jnp.float32), out_weight.astype(jnp.float32), up_weight.astype(jnp.float32), down_weight.astype(jnp.float32), norm_gain, norm_bias, attn_bias, res_bias, up_bias)
    result, puller = jax.vjp(forward, params, images.astype(jnp.float32))
    grads, images_grad = puller(out_cotangent.astype(jnp.float32))
    qkv_grad, outw_grad, upw_grad, downw_grad, gain_grad, nbias_grad, abias_grad, rbias_grad, ubias_grad = grads
    vector_params = (norm_gain, norm_bias, attn_bias, res_bias, up_bias)
    vector_moments = (gain_moment, nbias_moment, abias_moment, rbias_moment, ubias_moment)
    vector_grads = (gain_grad, nbias_grad, abias_grad, rbias_grad, ubias_grad)
    vmoment_new = [MOMENTUM * moment + gradient for moment, gradient in zip(vector_moments, vector_grads)]
    vparam_new = [param - VECTOR_RATE * moment for param, moment in zip(vector_params, vmoment_new)]
    qkv_mnew = MOMENTUM * qkv_moment + qkv_grad
    out_mnew = MOMENTUM * out_moment + outw_grad
    up_mnew = MOMENTUM * up_moment + upw_grad
    down_mnew = MOMENTUM * down_moment + downw_grad
    qkv_new = jnp.stack([muon_matrix(qkv_weight[:, column], qkv_mnew[:, column]) for column in range(3)], axis=1)
    out_new = muon_matrix(out_weight, out_mnew)
    up_new = muon_matrix(up_weight, up_mnew)
    down_new = muon_matrix(down_weight, down_mnew)
    return (result.astype(jnp.bfloat16), images_grad, qkv_grad, outw_grad, upw_grad, downw_grad, gain_grad, nbias_grad, abias_grad, rbias_grad, ubias_grad, qkv_new, out_new, up_new, down_new, vparam_new[0], vparam_new[1], vparam_new[2], vparam_new[3], vparam_new[4], qkv_mnew, out_mnew, up_mnew, down_mnew, vmoment_new[0], vmoment_new[1], vmoment_new[2], vmoment_new[3], vmoment_new[4])
```

```python
import math

import jax
import jax.numpy as jnp
from jax import lax
from jax.sharding import PartitionSpec as P

HEAD_DIM = 64
NS_STEPS = 5


HIGHEST = lax.Precision.HIGHEST
LN_EPS = 1e-06
NS_EPS = 1e-06
COEF_A = 3.4445
COEF_B = -4.775
COEF_C = 2.0315
MOMENTUM = 0.95
MUON_RATE = 0.15
VECTOR_RATE = 0.002
ROOT_HALF = 0.7071067811865476
ROOT_TWO_PI = 2.5066282746310002


PLANE = 4


def xor_pairs(count, bits):
    return [(index, index ^ bits) for index in range(count)]


def swap(block, bits):
    return lax.ppermute(block, "fsdp", xor_pairs(lax.axis_size("fsdp"), bits))


def place():
    rank = lax.axis_index("fsdp")
    return (rank % PLANE, rank // PLANE)


def put(buffer, piece, index, axis):
    return lax.dynamic_update_slice_in_dim(buffer, jnp.expand_dims(piece, axis), index, axis)


def pick(buffer, index, axis):
    return lax.dynamic_index_in_dim(buffer, index, axis, keepdims=False)


def gather_rows(shard):
    count = lax.axis_size("fsdp")
    layers = count // PLANE
    flat, layer = place()
    rows, cols = shard.shape
    half = cols // 2
    column = jnp.zeros((layers, rows, cols), shard.dtype)
    column = put(column, shard, layer, 0)
    for step in range(1, layers):
        column = put(column, swap(shard, PLANE * step), layer ^ step, 0)
    from_x = swap(column, 1)
    from_y = swap(column, 2)
    across_x = swap(from_x[:, :, :half], 2)
    across_y = swap(from_y[:, :, half:], 1)
    whole = jnp.zeros((layers, PLANE, rows, cols), shard.dtype)
    whole = put(whole, column, flat, 1)
    whole = put(whole, from_x, flat ^ 1, 1)
    whole = put(whole, from_y, flat ^ 2, 1)
    whole = put(whole, jnp.concatenate([across_x, across_y], axis=2), flat ^ 3, 1)
    return whole.reshape(count * rows, cols)


def wide(block):
    return block.astype(jnp.float32)


def scatter_sum(partial_sum):
    count = lax.axis_size("fsdp")
    layers = count // PLANE
    flat, layer = place()
    cols = partial_sum.shape[1]
    rows = partial_sum.shape[0] // count
    half = cols // 2
    low = partial_sum.astype(jnp.bfloat16).reshape(layers, PLANE, rows, cols)
    mine = pick(low, flat, 1)
    to_x = pick(low, flat ^ 1, 1)
    to_y = pick(low, flat ^ 2, 1)
    to_far = pick(low, flat ^ 3, 1)
    left = swap(to_far[:, :, :half], 1)
    right = swap(to_far[:, :, half:], 2)
    to_y = jnp.concatenate(
        [(wide(to_y[:, :, :half]) + wide(left)).astype(jnp.bfloat16), to_y[:, :, half:]], axis=2
    )
    to_x = jnp.concatenate(
        [to_x[:, :, :half], (wide(to_x[:, :, half:]) + wide(right)).astype(jnp.bfloat16)], axis=2
    )
    total = wide(mine) + wide(swap(to_x, 1)) + wide(swap(to_y, 2))
    total_low = total.astype(jnp.bfloat16)
    result = pick(total, layer, 0)
    for step in range(1, layers):
        result = result + wide(swap(pick(total_low, layer ^ step, 0), PLANE * step))
    return result


def total_everywhere(vector):
    bits = 1
    while bits < lax.axis_size("fsdp"):
        vector = vector + swap(vector, bits)
        bits *= 2
    return vector


def send(block, pairs):
    return lax.ppermute(block, ("fsdp", "tensor"), sorted(pairs))


def wide_owners(layers):
    return {
        (0, 0): PLANE * (1 % layers),
        (0, 1): PLANE * (2 % layers) + 1,
        (1, 0): PLANE * (2 % layers) + 3,
        (1, 1): PLANE * (1 % layers) + 2,
    }


def holds_up(flat, half):
    return (flat & 1) == half


def bring_wide(up_rows, down_rows):
    layers = lax.axis_size("fsdp") // PLANE
    owners = wide_owners(layers)
    flat, _ = place()
    keep_up = holds_up(flat, lax.axis_index("tensor"))
    kept = jnp.where(keep_up, up_rows, down_rows)
    sent = jnp.where(keep_up, down_rows, up_rows)
    kept = jnp.concatenate([kept, swap(sent, 1)], axis=0)
    pairs = []
    for (_, half), owner in owners.items():
        for layer in range(layers):
            target = PLANE * layer + owner % PLANE
            pairs.append(((target ^ 2) * 2 + half, target * 2 + half))
    kept = jnp.concatenate([kept, send(kept, pairs)], axis=0)
    pieces = [kept]
    for step in range(1, layers):
        pairs = [((o ^ (PLANE * step)) * 2 + half, o * 2 + half) for (_, half), o in owners.items()]
        pieces.append(send(kept, pairs))
    return jnp.concatenate(pieces, axis=0)


def return_wide(matrix):
    layers = lax.axis_size("fsdp") // PLANE
    owners = wide_owners(layers)
    flat, layer = place()
    half = lax.axis_index("tensor")
    plane_rows = matrix.shape[0] // layers
    rows = plane_rows // PLANE
    is_owner = owner_here()
    mine = jnp.where(is_owner, matrix[:plane_rows], jnp.zeros_like(matrix[:plane_rows]))
    for step in range(1, layers):
        pairs = [(o * 2 + side, (o ^ (PLANE * step)) * 2 + side) for (_, side), o in owners.items()]
        mine = mine + send(matrix[plane_rows * step : plane_rows * (step + 1)], pairs)
    blocks = [mine[rows * index : rows * (index + 1)] for index in range(PLANE)]
    found = [blocks[0]]
    for bits in range(1, PLANE):
        pairs = []
        for (_, side), owner in owners.items():
            for level in range(layers):
                source = PLANE * level + owner % PLANE
                pairs.append((source * 2 + side, (source ^ bits) * 2 + side))
        found.append(send(blocks[bits], pairs))
    found = jnp.stack(found)
    up_at = jnp.where(half == 0, owners[0, 0] % PLANE, owners[0, 1] % PLANE)
    down_at = jnp.where(half == 0, owners[1, 0] % PLANE, owners[1, 1] % PLANE)
    return (pick(found, flat ^ up_at, 0), pick(found, flat ^ down_at, 0))


def owner_here():
    owners = wide_owners(lax.axis_size("fsdp") // PLANE)
    rank = lax.axis_index("fsdp")
    half = lax.axis_index("tensor")
    answer = False
    for (_, side), owner in owners.items():
        answer = answer | ((rank == owner) & (half == side))
    return answer


def bring_narrow(blocks):
    layers = lax.axis_size("fsdp") // PLANE
    flat, _ = place()
    odd_x = (flat & 1) == 1
    odd_y = (flat & 2) == 2
    even = jnp.concatenate([blocks[0], blocks[2]], axis=0)
    odd = jnp.concatenate([blocks[1], blocks[3]], axis=0)
    kept = jnp.where(odd_x, odd, even)
    got = swap(jnp.where(odd_x, even, odd), 1)
    rows = blocks[0].shape[0]
    low_part = jnp.concatenate([kept[:rows], got[:rows]], axis=0)
    high_part = jnp.concatenate([kept[rows:], got[rows:]], axis=0)
    kept = jnp.where(odd_y, high_part, low_part)
    got = swap(jnp.where(odd_y, low_part, high_part), 2)
    kept = jnp.concatenate([kept, got], axis=0)
    return jnp.concatenate(
        [kept] + [swap(kept, PLANE * step) for step in range(1, layers)], axis=0
    )


def return_narrow(mine):
    flat, _ = place()
    rows = mine.shape[0] // PLANE
    blocks = [mine[rows * index : rows * (index + 1)] for index in range(PLANE)]
    found = jnp.stack([blocks[0]] + [swap(blocks[bits], bits) for bits in range(1, PLANE)])
    return [pick(found, flat ^ index, 0) for index in range(PLANE)]


def low_dot(left, right, dims):
    return lax.dot_general(
        left.astype(jnp.bfloat16),
        right.astype(jnp.bfloat16),
        (dims, ((), ())),
        preferred_element_type=jnp.float32,
    )


def orthogonal(matrix):
    count = matrix.shape[0]
    current = matrix.astype(jnp.float32)
    norm_value = jnp.sqrt(jnp.sum(current * current))
    current = current / (norm_value + NS_EPS)
    row = lax.broadcasted_iota(jnp.int32, (count, count), 0)
    on_diagonal = row == lax.broadcasted_iota(jnp.int32, (count, count), 1)
    for repeat in range(NS_STEPS):
        gram = low_dot(current, current, ((1,), (1,)))
        level = jnp.sum(current * current) / count
        rest = jnp.where(on_diagonal, gram - level, gram)
        square = low_dot(rest, rest, ((1,), (0,)))
        poly = (COEF_B + 2.0 * COEF_C * level) * rest + COEF_C * square
        keep = COEF_A + COEF_B * level + COEF_C * level * level
        current = keep * current + low_dot(poly, current, ((1,), (0,)))
    return current.astype(jnp.bfloat16)


def gelu_value(upper):
    return 0.5 * upper * (1.0 + jax.scipy.special.erf(upper * ROOT_HALF))


def gelu_slope(upper):
    return (
        0.5 * (1.0 + jax.scipy.special.erf(upper * ROOT_HALF))
        + upper * jnp.exp(-0.5 * upper * upper) / ROOT_TWO_PI
    )


def layer_stats(values):
    center = values - jnp.mean(values, axis=-1, keepdims=True)
    inverse = lax.rsqrt(jnp.mean(center * center, axis=-1, keepdims=True) + LN_EPS)
    return (center * inverse, inverse)


def norm_back(grad_out, normed, inverse, gain):
    scaled = grad_out * gain
    return inverse * (
        scaled
        - jnp.mean(scaled, axis=-1, keepdims=True)
        - normed * jnp.mean(scaled * normed, axis=-1, keepdims=True)
    )


def split_heads(block):
    return block.reshape(block.shape[0], 3, -1, HEAD_DIM)


def attend(block):
    parts = split_heads(block)
    scale = HEAD_DIM ** (-0.5)
    scores = (
        jnp.einsum("qhe,khe->hqk", parts[:, 0], parts[:, 1], preferred_element_type=jnp.float32)
        * scale
    )
    ceiling = jnp.max(scores, axis=-1, keepdims=True)
    exponent = jnp.exp(scores - ceiling)
    total = jnp.sum(exponent, axis=-1, keepdims=True)
    probs = exponent / total
    mixed = jnp.einsum(
        "hqk,khe->qhe", probs.astype(jnp.bfloat16), parts[:, 2], preferred_element_type=jnp.float32
    )
    return (mixed.reshape(block.shape[0], -1).astype(jnp.bfloat16), ceiling + jnp.log(total))


def attend_back(items):
    block, log_total, mixed_grad = items
    parts = split_heads(block)
    scale = HEAD_DIM ** (-0.5)
    query_part = parts[:, 0]
    key_part = parts[:, 1]
    value_part = parts[:, 2]
    scores = (
        jnp.einsum("qhe,khe->hqk", query_part, key_part, preferred_element_type=jnp.float32) * scale
    )
    probs = jnp.exp(scores - log_total)
    heads_grad = mixed_grad.reshape(mixed_grad.shape[0], -1, HEAD_DIM)
    prob_grad = jnp.einsum(
        "qhe,khe->hqk", heads_grad, value_part, preferred_element_type=jnp.float32
    )
    value_grad = jnp.einsum(
        "hqk,qhe->khe", probs.astype(jnp.bfloat16), heads_grad, preferred_element_type=jnp.float32
    )
    score_grad = (probs * (prob_grad - jnp.sum(probs * prob_grad, axis=-1, keepdims=True))).astype(
        jnp.bfloat16
    )
    query_grad = (
        jnp.einsum("hqk,khe->qhe", score_grad, key_part, preferred_element_type=jnp.float32) * scale
    )
    key_grad = (
        jnp.einsum("hqk,qhe->khe", score_grad, query_part, preferred_element_type=jnp.float32)
        * scale
    )
    stacked = jnp.stack([query_grad, key_grad, value_grad], axis=1)
    return stacked.reshape(block.shape[0], 3, -1).astype(jnp.bfloat16)


def tensor_total(partial_sum):
    return partial_sum + lax.ppermute(partial_sum, "tensor", [(0, 1), (1, 0)])


def body(
    images,
    out_cotangent,
    qkv_weight,
    out_weight,
    up_weight,
    down_weight,
    norm_gain,
    norm_bias,
    attn_bias,
    res_bias,
    up_bias,
    qkv_moment,
    out_moment,
    up_moment,
    down_moment,
    gain_moment,
    nbias_moment,
    abias_moment,
    rbias_moment,
    ubias_moment,
):
    shard_rows = qkv_weight.shape[0]
    head_width = qkv_weight.shape[2]
    first = jnp.concatenate([qkv_weight.reshape(shard_rows, -1), out_weight], axis=1)
    first = gather_rows(first)
    qkv_full = first[:, : 3 * head_width].reshape(-1, 3, head_width)
    out_full = first[:, 3 * head_width :]
    up_full = gather_rows(up_weight)
    down_full = gather_rows(down_weight)
    image_count, length, width = images.shape
    tokens = images.reshape(-1, width).astype(jnp.float32)
    hat_one, inv_one = layer_stats(tokens)
    normed1 = (hat_one * norm_gain[0] + norm_bias[0]).astype(jnp.bfloat16)
    proj = jnp.einsum("td,djh->tjh", normed1, qkv_full, preferred_element_type=jnp.float32)
    bias_three = jnp.stack([attn_bias[0], jnp.zeros_like(attn_bias[0]), attn_bias[1]])
    proj = (proj + bias_three).astype(jnp.bfloat16)
    proj_images = proj.reshape(image_count, length, 3, head_width)
    attended = [attend(proj_images[index]) for index in range(image_count)]
    attn_images = jnp.stack([item[0] for item in attended])
    attn_rows = attn_images.reshape(-1, head_width)
    branch = tensor_total(
        jnp.einsum("th,dh->td", attn_rows, out_full, preferred_element_type=jnp.float32)
    )
    mid = tokens + branch + res_bias[0]
    hat_two, inv_two = layer_stats(mid)
    normed2 = (hat_two * norm_gain[1] + norm_bias[1]).astype(jnp.bfloat16)
    upper = jnp.dot(normed2, up_full, preferred_element_type=jnp.float32) + up_bias
    hidden = gelu_value(upper).astype(jnp.bfloat16)
    second = tensor_total(
        jnp.einsum("tf,df->td", hidden, down_full, preferred_element_type=jnp.float32)
    )
    result = mid + second + res_bias[1]
    grad_top = out_cotangent.reshape(-1, width).astype(jnp.float32)
    top_low = grad_top.astype(jnp.bfloat16)
    downw_grad = jnp.einsum("td,tf->df", top_low, hidden, preferred_element_type=jnp.float32)
    hidden_grad = jnp.dot(top_low, down_full, preferred_element_type=jnp.float32)
    upper_grad = (hidden_grad * gelu_slope(upper)).astype(jnp.bfloat16)
    ubias_grad = jnp.sum(upper_grad, axis=0, dtype=jnp.float32)
    upw_grad = jnp.einsum("td,tf->df", normed2, upper_grad, preferred_element_type=jnp.float32)
    normed2_grad = tensor_total(
        jnp.einsum("tf,df->td", upper_grad, up_full, preferred_element_type=jnp.float32)
    )
    gain_two = jnp.sum(normed2_grad * hat_two, axis=0)
    shift_two = jnp.sum(normed2_grad, axis=0)
    mid_grad = grad_top + norm_back(normed2_grad, hat_two, inv_two, norm_gain[1])
    rbias_grad = jnp.stack([jnp.sum(mid_grad, axis=0), jnp.sum(grad_top, axis=0)])
    mid_low = mid_grad.astype(jnp.bfloat16)
    outw_grad = jnp.einsum("td,th->dh", mid_low, attn_rows, preferred_element_type=jnp.float32)
    attn_grad = jnp.dot(mid_low, out_full, preferred_element_type=jnp.float32).astype(jnp.bfloat16)
    mixed_grads = attn_grad.reshape(image_count, length, head_width)
    proj_grad = jnp.stack(
        [
            attend_back((proj_images[index], attended[index][1], mixed_grads[index]))
            for index in range(image_count)
        ]
    )
    proj_grad = proj_grad.reshape(-1, 3, head_width)
    qkv_grad = jnp.einsum("td,tjh->djh", normed1, proj_grad, preferred_element_type=jnp.float32)
    abias_grad = jnp.stack(
        [
            jnp.sum(proj_grad[:, 0], axis=0, dtype=jnp.float32),
            jnp.sum(proj_grad[:, 2], axis=0, dtype=jnp.float32),
        ]
    )
    normed1_grad = tensor_total(
        jnp.einsum("tjh,djh->td", proj_grad, qkv_full, preferred_element_type=jnp.float32)
    )
    gain_one = jnp.sum(normed1_grad * hat_one, axis=0)
    shift_one = jnp.sum(normed1_grad, axis=0)
    input_grad = mid_grad + norm_back(normed1_grad, hat_one, inv_one, norm_gain[0])
    gain_grad = jnp.stack([gain_one, gain_two])
    nbias_grad = jnp.stack([shift_one, shift_two])
    down_shard = scatter_sum(downw_grad)
    up_shard = scatter_sum(upw_grad)
    first_shard = scatter_sum(
        jnp.concatenate([qkv_grad.reshape(width, -1), outw_grad], axis=1)
    )
    grad_shards = (
        first_shard[:, : 3 * head_width].reshape(shard_rows, 3, head_width),
        first_shard[:, 3 * head_width :],
        up_shard,
        down_shard,
    )
    vector_list = (gain_grad, nbias_grad, abias_grad, rbias_grad, ubias_grad)
    packed = jnp.concatenate([item.reshape(-1, 128) for item in vector_list], axis=0)
    packed = total_everywhere(packed)
    vector_grads = []
    start = 0
    for item in vector_list:
        lines = item.size // 128
        vector_grads.append(packed[start : start + lines].reshape(item.shape))
        start += lines
    moment_shards = tuple(
        (
            MOMENTUM * stored + gradient
            for stored, gradient in zip(
                (qkv_moment, out_moment, up_moment, down_moment), grad_shards
            )
        )
    )
    shard_low = tuple((stored.astype(jnp.bfloat16) for stored in moment_shards))
    weight_shards = [
        qkv_weight[:, 0],
        qkv_weight[:, 1],
        qkv_weight[:, 2],
        out_weight,
        up_weight,
        down_weight,
    ]
    wide_block = bring_wide(shard_low[2], shard_low[3])
    wide_orth = lax.cond(owner_here(), orthogonal, jnp.zeros_like, wide_block)
    up_orth, down_orth = return_wide(wide_orth)
    narrow_block = bring_narrow(
        [shard_low[0][:, 0], shard_low[0][:, 1], shard_low[0][:, 2], shard_low[1]]
    )
    plane_rows = PLANE * shard_rows
    narrow_orth = orthogonal(narrow_block.T).T[:plane_rows]
    pieces = return_narrow(narrow_orth) + [up_orth, down_orth]
    updated = []
    for stored, piece in zip(weight_shards, pieces):
        factor = 0.2 * math.sqrt(max(width, piece.shape[1]))
        updated.append(stored.astype(jnp.float32) - MUON_RATE * (piece.astype(jnp.float32) * factor))
    qkv_new = jnp.stack(updated[:3], axis=1)
    out_new = updated[3]
    up_new = updated[4]
    down_new = updated[5]
    vector_params = (norm_gain, norm_bias, attn_bias, res_bias, up_bias)
    vector_moments = (gain_moment, nbias_moment, abias_moment, rbias_moment, ubias_moment)
    vmoment_new = [
        MOMENTUM * stored + gradient for stored, gradient in zip(vector_moments, vector_grads)
    ]
    vparam_new = [param - VECTOR_RATE * stored for param, stored in zip(vector_params, vmoment_new)]
    block_out = result.reshape(image_count, length, width).astype(jnp.bfloat16)
    images_grad = input_grad.reshape(image_count, length, width)
    return (
        block_out,
        images_grad,
        grad_shards[0],
        grad_shards[1],
        grad_shards[2],
        grad_shards[3],
        vector_grads[0],
        vector_grads[1],
        vector_grads[2],
        vector_grads[3],
        vector_grads[4],
        qkv_new,
        out_new,
        up_new,
        down_new,
        vparam_new[0],
        vparam_new[1],
        vparam_new[2],
        vparam_new[3],
        vparam_new[4],
        moment_shards[0],
        moment_shards[1],
        moment_shards[2],
        moment_shards[3],
        vmoment_new[0],
        vmoment_new[1],
        vmoment_new[2],
        vmoment_new[3],
        vmoment_new[4],
    )


def solution(mesh):
    placed = (
        P("fsdp", None, None),
        P("fsdp", None, None),
        P("fsdp", None, "tensor"),
        P("fsdp", "tensor"),
        P("fsdp", "tensor"),
        P("fsdp", "tensor"),
        P(),
        P(),
        P(None, "tensor"),
        P(),
        P("tensor"),
        P("fsdp", None, "tensor"),
        P("fsdp", "tensor"),
        P("fsdp", "tensor"),
        P("fsdp", "tensor"),
        P(),
        P(),
        P(None, "tensor"),
        P(),
        P("tensor"),
    )
    return jax.shard_map(
        body,
        mesh=mesh,
        in_specs=placed,
        out_specs=(
            P("fsdp", None, None),
            P("fsdp", None, None),
            P("fsdp", None, "tensor"),
            P("fsdp", "tensor"),
            P("fsdp", "tensor"),
            P("fsdp", "tensor"),
            P(),
            P(),
            P(None, "tensor"),
            P(),
            P("tensor"),
            P("fsdp", None, "tensor"),
            P("fsdp", "tensor"),
            P("fsdp", "tensor"),
            P("fsdp", "tensor"),
            P(),
            P(),
            P(None, "tensor"),
            P(),
            P("tensor"),
            P("fsdp", None, "tensor"),
            P("fsdp", "tensor"),
            P("fsdp", "tensor"),
            P("fsdp", "tensor"),
            P(),
            P(),
            P(None, "tensor"),
            P(),
            P("tensor"),
        ),
        check_vma=False,
    )
```

```python
import functools
import math

import jax
import jax.numpy as jnp
from jax import lax
from jax.experimental import pallas as pl
from jax.experimental.pallas import tpu as pltpu
from jax.sharding import PartitionSpec as P

HEAD_DIM = 64
NS_STEPS = 5


HIGHEST = lax.Precision.HIGHEST
LN_EPS = 1e-06
NS_EPS = 1e-06
COEF_A = 3.4445
COEF_B = -4.775
COEF_C = 2.0315
MOMENTUM = 0.95
MUON_RATE = 0.15
VECTOR_RATE = 0.002
ROOT_HALF = 0.7071067811865476
ROOT_TWO_PI = 2.5066282746310002


PLANE = 4


def xor_pairs(count, bits):
    return [(index, index ^ bits) for index in range(count)]


def swap(block, bits):
    return lax.ppermute(block, "fsdp", xor_pairs(lax.axis_size("fsdp"), bits))


def place():
    rank = lax.axis_index("fsdp")
    return (rank % PLANE, rank // PLANE)


def put(buffer, piece, index, axis):
    return lax.dynamic_update_slice_in_dim(buffer, jnp.expand_dims(piece, axis), index, axis)


def pick(buffer, index, axis):
    return lax.dynamic_index_in_dim(buffer, index, axis, keepdims=False)


def gather_rows(shards, after=None):
    count = lax.axis_size("fsdp")
    layers = count // PLANE
    flat, layer = place()
    shard = jnp.concatenate(shards, axis=1) if len(shards) > 1 else shards[0]
    if after is not None:
        shard, _ = lax.optimization_barrier((shard, after))
    rows, cols = shard.shape
    half = cols // 256 * 128
    column = jnp.zeros((layers, rows, cols), shard.dtype)
    column = put(column, shard, layer, 0)
    for step in range(1, layers):
        column = put(column, swap(shard, PLANE * step), layer ^ step, 0)
    from_x = swap(column, 1)
    from_y = swap(column, 2)
    across_x = swap(from_x[:, :, :half], 2)
    across_y = swap(from_y[:, :, half:], 1)
    far = jnp.concatenate([across_x, across_y], axis=2)
    results = []
    start = 0
    for item in shards:
        stop = start + item.shape[1]
        whole = jnp.zeros((layers, PLANE, rows, item.shape[1]), shard.dtype)
        whole = put(whole, column[:, :, start:stop], flat, 1)
        whole = put(whole, from_x[:, :, start:stop], flat ^ 1, 1)
        whole = put(whole, from_y[:, :, start:stop], flat ^ 2, 1)
        whole = put(whole, far[:, :, start:stop], flat ^ 3, 1)
        results.append(whole.reshape(count * rows, item.shape[1]))
        start = stop
    return (results, (from_x, from_y))


def wide(block):
    return block.astype(jnp.float32)


def join(pieces):
    return jnp.concatenate(pieces, axis=-1) if len(pieces) > 1 else pieces[0]


def scatter_begin(partial_sums):
    count = lax.axis_size("fsdp")
    layers = count // PLANE
    flat, _ = place()
    rows = partial_sums[0].shape[0] // count
    lows = [
        item.astype(jnp.bfloat16).reshape(layers, PLANE, rows, item.shape[1])
        for item in partial_sums
    ]
    mine, to_x, to_y, to_far = [
        join([pick(item, flat ^ bits, 1) for item in lows]) for bits in range(PLANE)
    ]
    half = mine.shape[2] // 256 * 128
    left = swap(to_far[:, :, :half], 1)
    right = swap(to_far[:, :, half:], 2)
    return (mine, to_x, to_y, left, right)


def scatter_middle(state):
    mine, to_x, to_y, left, right = state
    half = left.shape[2]
    to_y = jnp.concatenate(
        [(wide(to_y[:, :, :half]) + wide(left)).astype(jnp.bfloat16), to_y[:, :, half:]], axis=2
    )
    to_x = jnp.concatenate(
        [to_x[:, :, :half], (wide(to_x[:, :, half:]) + wide(right)).astype(jnp.bfloat16)], axis=2
    )
    return (mine, swap(to_x, 1), swap(to_y, 2))


def scatter_end(state):
    mine, from_x, from_y = state
    layers = lax.axis_size("fsdp") // PLANE
    _, layer = place()
    total = wide(mine) + wide(from_x) + wide(from_y)
    total_low = total.astype(jnp.bfloat16)
    result = pick(total, layer, 0)
    for step in range(1, layers):
        result = result + wide(swap(pick(total_low, layer ^ step, 0), PLANE * step))
    return result


def scatter_sum(partial_sums):
    return scatter_end(scatter_middle(scatter_begin(partial_sums)))


def total_everywhere(vector):
    bits = 1
    while bits < lax.axis_size("fsdp"):
        vector = vector + swap(vector, bits)
        bits *= 2
    return vector


def send(block, pairs):
    return lax.ppermute(block, ("fsdp", "tensor"), sorted(pairs))


def wide_owners(layers):
    return {
        (0, 0): PLANE * (1 % layers),
        (0, 1): PLANE * (2 % layers) + 1,
        (1, 0): PLANE * (2 % layers) + 3,
        (1, 1): PLANE * (1 % layers) + 2,
    }


def holds_up(flat, half):
    return (flat & 1) == half


def bring_wide(up_rows, down_rows):
    layers = lax.axis_size("fsdp") // PLANE
    owners = wide_owners(layers)
    flat, _ = place()
    keep_up = holds_up(flat, lax.axis_index("tensor"))
    kept = jnp.where(keep_up, up_rows, down_rows)
    sent = jnp.where(keep_up, down_rows, up_rows)
    kept = jnp.concatenate([kept, swap(sent, 1)], axis=0)
    pairs = []
    for (_, half), owner in owners.items():
        for layer in range(layers):
            target = PLANE * layer + owner % PLANE
            pairs.append(((target ^ 2) * 2 + half, target * 2 + half))
    kept = jnp.concatenate([kept, send(kept, pairs)], axis=0)
    pieces = [kept]
    for step in range(1, layers):
        pairs = [((o ^ (PLANE * step)) * 2 + half, o * 2 + half) for (_, half), o in owners.items()]
        pieces.append(send(kept, pairs))
    return jnp.concatenate(pieces, axis=0)


def return_wide(matrix):
    layers = lax.axis_size("fsdp") // PLANE
    owners = wide_owners(layers)
    flat, layer = place()
    half = lax.axis_index("tensor")
    plane_rows = matrix.shape[0] // layers
    rows = plane_rows // PLANE
    is_owner = owner_here()
    mine = jnp.where(is_owner, matrix[:plane_rows], jnp.zeros_like(matrix[:plane_rows]))
    for step in range(1, layers):
        pairs = [(o * 2 + side, (o ^ (PLANE * step)) * 2 + side) for (_, side), o in owners.items()]
        mine = mine + send(matrix[plane_rows * step : plane_rows * (step + 1)], pairs)
    blocks = [mine[rows * index : rows * (index + 1)] for index in range(PLANE)]
    found = [blocks[0]]
    for bits in range(1, PLANE):
        pairs = []
        for (_, side), owner in owners.items():
            for level in range(layers):
                source = PLANE * level + owner % PLANE
                pairs.append((source * 2 + side, (source ^ bits) * 2 + side))
        found.append(send(blocks[bits], pairs))
    found = jnp.stack(found)
    up_at = jnp.where(half == 0, owners[0, 0] % PLANE, owners[0, 1] % PLANE)
    down_at = jnp.where(half == 0, owners[1, 0] % PLANE, owners[1, 1] % PLANE)
    return (pick(found, flat ^ up_at, 0), pick(found, flat ^ down_at, 0))


def owner_here():
    owners = wide_owners(lax.axis_size("fsdp") // PLANE)
    rank = lax.axis_index("fsdp")
    half = lax.axis_index("tensor")
    answer = False
    for (_, side), owner in owners.items():
        answer = answer | ((rank == owner) & (half == side))
    return answer


def bring_narrow(blocks):
    layers = lax.axis_size("fsdp") // PLANE
    flat, _ = place()
    odd_x = (flat & 1) == 1
    odd_y = (flat & 2) == 2
    even = jnp.concatenate([blocks[0], blocks[2]], axis=0)
    odd = jnp.concatenate([blocks[1], blocks[3]], axis=0)
    kept = jnp.where(odd_x, odd, even)
    got = swap(jnp.where(odd_x, even, odd), 1)
    rows = blocks[0].shape[0]
    low_part = jnp.concatenate([kept[:rows], got[:rows]], axis=0)
    high_part = jnp.concatenate([kept[rows:], got[rows:]], axis=0)
    kept = jnp.where(odd_y, high_part, low_part)
    got = swap(jnp.where(odd_y, low_part, high_part), 2)
    kept = jnp.concatenate([kept, got], axis=0)
    return jnp.concatenate(
        [kept] + [swap(kept, PLANE * step) for step in range(1, layers)], axis=0
    )


def return_narrow(mine):
    flat, _ = place()
    rows = mine.shape[0] // PLANE
    blocks = [mine[rows * index : rows * (index + 1)] for index in range(PLANE)]
    found = jnp.stack([blocks[0]] + [swap(blocks[bits], bits) for bits in range(1, PLANE)])
    return [pick(found, flat ^ index, 0) for index in range(PLANE)]


def low_dot(left, right, dims):
    return lax.dot_general(
        left.astype(jnp.bfloat16),
        right.astype(jnp.bfloat16),
        (dims, ((), ())),
        preferred_element_type=jnp.float32,
    )


STRIP = 256


def orth_kernel(steps, is_first, is_last, active_ref, block_ref, out_ref, *scratch):
    low, rest, rest_low, poly = scratch[:4]
    current = scratch[4] if is_last else out_ref
    count = block_ref.shape[0]
    strips = count // STRIP

    def strip(index):
        return pl.ds(pl.multiple_of(index * STRIP, STRIP), STRIP)

    @pl.when(active_ref[0] > 0)
    def _():
        def measure(index, total):
            piece = block_ref[strip(index), :].astype(jnp.float32)
            return total + jnp.sum(piece * piece)

        if is_first:
            squares = lax.fori_loop(0, strips, measure, jnp.float32(0.0))
            norm = jnp.sqrt(jnp.full((1, 128), squares, jnp.float32)) + NS_EPS

        def scale(index, total):
            piece = block_ref[strip(index), :].astype(jnp.float32)
            if is_first:
                piece = piece / norm[:, :1]
            current[strip(index), :] = piece
            low[strip(index), :] = piece.astype(jnp.bfloat16)
            return total + jnp.sum(piece * piece)

        squares = lax.fori_loop(0, strips, scale, jnp.float32(0.0))

        def step(_, squares):
            level = squares * (1.0 / count)

            def gram(index, carry):
                part = low_dot(low[strip(index), :], low[...], ((1,), (1,)))
                row = lax.broadcasted_iota(jnp.int32, part.shape, 0) + index * STRIP
                col = lax.broadcasted_iota(jnp.int32, part.shape, 1)
                part = jnp.where(row == col, part - level, part)
                rest[strip(index), :] = part
                rest_low[strip(index), :] = part.astype(jnp.bfloat16)
                return carry

            lax.fori_loop(0, strips, gram, 0)

            def square(index, carry):
                part = low_dot(rest_low[strip(index), :], rest_low[...], ((1,), (0,)))
                part = (COEF_B + 2.0 * COEF_C * level) * rest[strip(index), :] + COEF_C * part
                poly[strip(index), :] = part.astype(jnp.bfloat16)
                return carry

            lax.fori_loop(0, strips, square, 0)
            keep = COEF_A + COEF_B * level + COEF_C * level * level

            def advance(index, total):
                piece = keep * current[strip(index), :] + low_dot(
                    poly[strip(index), :], low[...], ((1,), (0,))
                )
                current[strip(index), :] = piece
                return total + jnp.sum(piece * piece)

            squares = lax.fori_loop(0, strips, advance, jnp.float32(0.0))

            def round_low(index, carry):
                low[strip(index), :] = current[strip(index), :].astype(jnp.bfloat16)
                return carry

            lax.fori_loop(0, strips, round_low, 0)
            return squares

        lax.fori_loop(0, steps, step, squares)
        if is_last:

            def leave(index, carry):
                out_ref[strip(index), :] = low[strip(index), :]
                return carry

            lax.fori_loop(0, strips, leave, 0)


def orthogonal(matrix, active, steps=NS_STEPS, is_first=True, is_last=True):
    rows, cols = matrix.shape
    work = steps * 2 * rows * rows * (2 * cols + rows)
    scratch = [
        pltpu.VMEM((rows, cols), jnp.bfloat16),
        pltpu.VMEM((rows, rows), jnp.float32),
        pltpu.VMEM((rows, rows), jnp.bfloat16),
        pltpu.VMEM((rows, rows), jnp.bfloat16),
    ]
    if is_last:
        scratch.append(pltpu.VMEM((rows, cols), jnp.float32))
    return pl.pallas_call(
        functools.partial(orth_kernel, steps, is_first, is_last),
        out_shape=jax.ShapeDtypeStruct((rows, cols), jnp.bfloat16 if is_last else jnp.float32),
        in_specs=[
            pl.BlockSpec(memory_space=pltpu.SMEM),
            pl.BlockSpec(memory_space=pltpu.VMEM),
        ],
        out_specs=pl.BlockSpec(memory_space=pltpu.VMEM),
        scratch_shapes=scratch,
        compiler_params=pltpu.CompilerParams(vmem_limit_bytes=42 * 1024 * 1024),
        cost_estimate=pl.CostEstimate(
            flops=work, bytes_accessed=4 * rows * cols, transcendentals=0
        ),
        name="orth",
    )(active, matrix)


def gelu_value(upper):
    return 0.5 * upper * (1.0 + jax.scipy.special.erf(upper * ROOT_HALF))


def gelu_slope(upper):
    return (
        0.5 * (1.0 + jax.scipy.special.erf(upper * ROOT_HALF))
        + upper * jnp.exp(-0.5 * upper * upper) / ROOT_TWO_PI
    )


def layer_stats(values):
    center = values - jnp.mean(values, axis=-1, keepdims=True)
    inverse = lax.rsqrt(jnp.mean(center * center, axis=-1, keepdims=True) + LN_EPS)
    return (center * inverse, inverse)


def norm_back(grad_out, normed, inverse, gain):
    scaled = grad_out * gain
    return inverse * (
        scaled
        - jnp.mean(scaled, axis=-1, keepdims=True)
        - normed * jnp.mean(scaled * normed, axis=-1, keepdims=True)
    )


def split_heads(block):
    return block.reshape(block.shape[0], 3, -1, HEAD_DIM)


def attend(block):
    parts = split_heads(block)
    scale = HEAD_DIM ** (-0.5)
    scores = (
        jnp.einsum("qhe,khe->hqk", parts[:, 0], parts[:, 1], preferred_element_type=jnp.float32)
        * scale
    )
    ceiling = jnp.max(scores, axis=-1, keepdims=True)
    exponent = jnp.exp(scores - ceiling)
    total = jnp.sum(exponent, axis=-1, keepdims=True)
    probs = exponent / total
    mixed = jnp.einsum(
        "hqk,khe->qhe", probs.astype(jnp.bfloat16), parts[:, 2], preferred_element_type=jnp.float32
    )
    return (mixed.reshape(block.shape[0], -1).astype(jnp.bfloat16), ceiling + jnp.log(total))


def attend_back(items):
    block, log_total, mixed_grad = items
    parts = split_heads(block)
    scale = HEAD_DIM ** (-0.5)
    query_part = parts[:, 0]
    key_part = parts[:, 1]
    value_part = parts[:, 2]
    scores = (
        jnp.einsum("qhe,khe->hqk", query_part, key_part, preferred_element_type=jnp.float32) * scale
    )
    probs = jnp.exp(scores - log_total)
    heads_grad = mixed_grad.reshape(mixed_grad.shape[0], -1, HEAD_DIM)
    prob_grad = jnp.einsum(
        "qhe,khe->hqk", heads_grad, value_part, preferred_element_type=jnp.float32
    )
    value_grad = jnp.einsum(
        "hqk,qhe->khe", probs.astype(jnp.bfloat16), heads_grad, preferred_element_type=jnp.float32
    )
    score_grad = (probs * (prob_grad - jnp.sum(probs * prob_grad, axis=-1, keepdims=True))).astype(
        jnp.bfloat16
    )
    query_grad = (
        jnp.einsum("hqk,khe->qhe", score_grad, key_part, preferred_element_type=jnp.float32) * scale
    )
    key_grad = (
        jnp.einsum("hqk,qhe->khe", score_grad, query_part, preferred_element_type=jnp.float32)
        * scale
    )
    stacked = jnp.stack([query_grad, key_grad, value_grad], axis=1)
    return stacked.reshape(block.shape[0], 3, -1).astype(jnp.bfloat16)


def tensor_total(partial_sum):
    return partial_sum + lax.ppermute(partial_sum, "tensor", [(0, 1), (1, 0)])


def body(
    images,
    out_cotangent,
    qkv_weight,
    out_weight,
    up_weight,
    down_weight,
    norm_gain,
    norm_bias,
    attn_bias,
    res_bias,
    up_bias,
    qkv_moment,
    out_moment,
    up_moment,
    down_moment,
    gain_moment,
    nbias_moment,
    abias_moment,
    rbias_moment,
    ubias_moment,
):
    shard_rows = qkv_weight.shape[0]
    head_width = qkv_weight.shape[2]
    (qkv_full,), mark = gather_rows([qkv_weight.reshape(shard_rows, -1)])
    (out_full, up_full), mark = gather_rows([out_weight, up_weight], mark)
    (down_full,), mark = gather_rows([down_weight], mark)
    image_count, length, width = images.shape
    tokens = images.reshape(-1, width).astype(jnp.float32)
    hat_one, inv_one = layer_stats(tokens)
    normed1 = (hat_one * norm_gain[0] + norm_bias[0]).astype(jnp.bfloat16)
    proj = jnp.dot(normed1, qkv_full, preferred_element_type=jnp.float32)
    bias_three = jnp.stack([attn_bias[0], jnp.zeros_like(attn_bias[0]), attn_bias[1]])
    proj = (proj + bias_three.reshape(1, -1)).astype(jnp.bfloat16)
    proj_images = proj.reshape(image_count, length, 3, head_width)
    attended = [attend(proj_images[index]) for index in range(image_count)]
    attn_images = jnp.stack([item[0] for item in attended])
    attn_rows = attn_images.reshape(-1, head_width)
    branch = tensor_total(
        jnp.einsum("th,dh->td", attn_rows, out_full, preferred_element_type=jnp.float32)
    )
    mid = tokens + branch + res_bias[0]
    hat_two, inv_two = layer_stats(mid)
    normed2 = (hat_two * norm_gain[1] + norm_bias[1]).astype(jnp.bfloat16)
    upper = jnp.dot(normed2, up_full, preferred_element_type=jnp.float32) + up_bias
    hidden = gelu_value(upper).astype(jnp.bfloat16)
    second = tensor_total(
        jnp.einsum("tf,df->td", hidden, down_full, preferred_element_type=jnp.float32)
    )
    result = mid + second + res_bias[1]
    grad_top = out_cotangent.reshape(-1, width).astype(jnp.float32)
    top_low = grad_top.astype(jnp.bfloat16)
    downw_grad = jnp.einsum("td,tf->df", top_low, hidden, preferred_element_type=jnp.float32)
    hidden_grad = jnp.dot(top_low, down_full, preferred_element_type=jnp.float32)
    upper_grad = (hidden_grad * gelu_slope(upper)).astype(jnp.bfloat16)
    ubias_grad = jnp.sum(upper_grad, axis=0, dtype=jnp.float32)
    upw_grad = jnp.einsum("td,tf->df", normed2, upper_grad, preferred_element_type=jnp.float32)
    upw_grad, upper_grad = lax.optimization_barrier((upw_grad.astype(jnp.bfloat16), upper_grad))
    normed2_grad = tensor_total(
        jnp.einsum("tf,df->td", upper_grad, up_full, preferred_element_type=jnp.float32)
    )
    gain_two = jnp.sum(normed2_grad * hat_two, axis=0)
    shift_two = jnp.sum(normed2_grad, axis=0)
    mid_grad = grad_top + norm_back(normed2_grad, hat_two, inv_two, norm_gain[1])
    rbias_grad = jnp.stack([jnp.sum(mid_grad, axis=0), jnp.sum(grad_top, axis=0)])
    mid_low = mid_grad.astype(jnp.bfloat16)
    outw_grad = jnp.einsum("td,th->dh", mid_low, attn_rows, preferred_element_type=jnp.float32)
    outw_grad, mid_low = lax.optimization_barrier((outw_grad.astype(jnp.bfloat16), mid_low))
    attn_grad = jnp.dot(mid_low, out_full, preferred_element_type=jnp.float32).astype(jnp.bfloat16)
    mixed_grads = attn_grad.reshape(image_count, length, head_width)
    proj_grad = jnp.stack(
        [
            attend_back((proj_images[index], attended[index][1], mixed_grads[index]))
            for index in range(image_count)
        ]
    )
    proj_grad = proj_grad.reshape(-1, 3, head_width)
    flat_grad = proj_grad.reshape(-1, 3 * head_width)
    qkv_grad = jnp.einsum("td,th->dh", normed1, flat_grad, preferred_element_type=jnp.float32)
    abias_grad = jnp.stack(
        [
            jnp.sum(proj_grad[:, 0], axis=0, dtype=jnp.float32),
            jnp.sum(proj_grad[:, 2], axis=0, dtype=jnp.float32),
        ]
    )
    normed1_grad = tensor_total(
        jnp.einsum("th,dh->td", flat_grad, qkv_full, preferred_element_type=jnp.float32)
    )
    gain_one = jnp.sum(normed1_grad * hat_one, axis=0)
    shift_one = jnp.sum(normed1_grad, axis=0)
    input_grad = mid_grad + norm_back(normed1_grad, hat_one, inv_one, norm_gain[0])
    gain_grad = jnp.stack([gain_one, gain_two])
    nbias_grad = jnp.stack([shift_one, shift_two])
    down_shard = scatter_sum([downw_grad])
    middle_shard = scatter_sum([outw_grad, upw_grad])
    out_shard = middle_shard[:, :head_width]
    up_shard = middle_shard[:, head_width:]
    up_new_moment = MOMENTUM * up_moment + up_shard
    down_new_moment = MOMENTUM * down_moment + down_shard
    wide_block = bring_wide(
        up_new_moment.astype(jnp.bfloat16), down_new_moment.astype(jnp.bfloat16)
    )
    owns = jnp.reshape(owner_here(), (1,)).astype(jnp.int32)
    qkv_shard = scatter_sum([qkv_grad])
    wide_orth = orthogonal(wide_block, owns)
    grad_shards = (
        qkv_shard.reshape(shard_rows, 3, head_width),
        out_shard,
        up_shard,
        down_shard,
    )
    vector_list = (gain_grad, nbias_grad, abias_grad, rbias_grad, ubias_grad)
    packed = jnp.concatenate([item.reshape(-1, 128) for item in vector_list], axis=0)
    packed = total_everywhere(packed)
    vector_grads = []
    start = 0
    for item in vector_list:
        lines = item.size // 128
        vector_grads.append(packed[start : start + lines].reshape(item.shape))
        start += lines
    moment_shards = (
        MOMENTUM * qkv_moment + grad_shards[0],
        MOMENTUM * out_moment + out_shard,
        up_new_moment,
        down_new_moment,
    )
    shard_low = tuple((stored.astype(jnp.bfloat16) for stored in moment_shards))
    weight_shards = [
        qkv_weight[:, 0],
        qkv_weight[:, 1],
        qkv_weight[:, 2],
        out_weight,
        up_weight,
        down_weight,
    ]
    up_orth, down_orth = return_wide(wide_orth)
    narrow_block = bring_narrow(
        [shard_low[0][:, 0], shard_low[0][:, 1], shard_low[0][:, 2], shard_low[1]]
    )
    plane_rows = PLANE * shard_rows
    narrow_orth = orthogonal(narrow_block.T, jnp.ones((1,), jnp.int32))[:, :plane_rows].T
    pieces = return_narrow(narrow_orth) + [up_orth, down_orth]
    updated = []
    for stored, piece in zip(weight_shards, pieces):
        factor = 0.2 * math.sqrt(max(width, piece.shape[1]))
        updated.append(stored.astype(jnp.float32) - MUON_RATE * (piece.astype(jnp.float32) * factor))
    qkv_new = jnp.stack(updated[:3], axis=1)
    out_new = updated[3]
    up_new = updated[4]
    down_new = updated[5]
    vector_params = (norm_gain, norm_bias, attn_bias, res_bias, up_bias)
    vector_moments = (gain_moment, nbias_moment, abias_moment, rbias_moment, ubias_moment)
    vmoment_new = [
        MOMENTUM * stored + gradient for stored, gradient in zip(vector_moments, vector_grads)
    ]
    vparam_new = [param - VECTOR_RATE * stored for param, stored in zip(vector_params, vmoment_new)]
    block_out = result.reshape(image_count, length, width).astype(jnp.bfloat16)
    images_grad = input_grad.reshape(image_count, length, width)
    return (
        block_out,
        images_grad,
        grad_shards[0],
        grad_shards[1],
        grad_shards[2],
        grad_shards[3],
        vector_grads[0],
        vector_grads[1],
        vector_grads[2],
        vector_grads[3],
        vector_grads[4],
        qkv_new,
        out_new,
        up_new,
        down_new,
        vparam_new[0],
        vparam_new[1],
        vparam_new[2],
        vparam_new[3],
        vparam_new[4],
        moment_shards[0],
        moment_shards[1],
        moment_shards[2],
        moment_shards[3],
        vmoment_new[0],
        vmoment_new[1],
        vmoment_new[2],
        vmoment_new[3],
        vmoment_new[4],
    )


def solution(mesh):
    placed = (
        P("fsdp", None, None),
        P("fsdp", None, None),
        P("fsdp", None, "tensor"),
        P("fsdp", "tensor"),
        P("fsdp", "tensor"),
        P("fsdp", "tensor"),
        P(),
        P(),
        P(None, "tensor"),
        P(),
        P("tensor"),
        P("fsdp", None, "tensor"),
        P("fsdp", "tensor"),
        P("fsdp", "tensor"),
        P("fsdp", "tensor"),
        P(),
        P(),
        P(None, "tensor"),
        P(),
        P("tensor"),
    )
    return jax.shard_map(
        body,
        mesh=mesh,
        in_specs=placed,
        out_specs=(
            P("fsdp", None, None),
            P("fsdp", None, None),
            P("fsdp", None, "tensor"),
            P("fsdp", "tensor"),
            P("fsdp", "tensor"),
            P("fsdp", "tensor"),
            P(),
            P(),
            P(None, "tensor"),
            P(),
            P("tensor"),
            P("fsdp", None, "tensor"),
            P("fsdp", "tensor"),
            P("fsdp", "tensor"),
            P("fsdp", "tensor"),
            P(),
            P(),
            P(None, "tensor"),
            P(),
            P("tensor"),
            P("fsdp", None, "tensor"),
            P("fsdp", "tensor"),
            P("fsdp", "tensor"),
            P("fsdp", "tensor"),
            P(),
            P(),
            P(None, "tensor"),
            P(),
            P("tensor"),
        ),
        check_vma=False,
    )
```
